128 devices in a mesh: dp: 64 (over z, y_hi, x, core), mp: 2 (over y_lo).
Axes of the slice: x: 4, y: 4 (y_hi: 2, y_lo: 2; y = y_hi * 2 + y_lo), z: 4, core: 2. Of those that a mesh axis runs over, the one named last changes fastest.
Arguments:
- tokens: bfloat16 [25600, 1792], P('dp', 'mp'), may hold values from -6 to 6
- cotangent: bfloat16 [25600, 1792], P('dp', 'mp'), may hold values from -6 to 6
- master: float32 [1792, 4, 1792], P('dp', None, 'mp')
- moment_one: float32 [1792, 4, 1792], P('dp', None, 'mp'), may hold values from -4 to 4
- moment_two: float32 [1792, 4, 1792], P('dp', None, 'mp'), may hold values from 0.01 to 1
- ln_gain: float32 [1792], replicated, may hold values from 0.1 to 1.9
- ln_bias: float32 [1792], replicated, may hold values from -3 to 3
- norm_moment_one: float32 [2, 1792], replicated, may hold values from -4 to 4
- norm_moment_two: float32 [2, 1792], replicated, may hold values from 0.01 to 1
- image_count: int32 [64], P('dp'), may hold values from 1 to 25, as said below
- tokens_per_image: int32 [64], P('dp'), may hold values from 16 to 400, as said below
Outputs:
- block_out: bfloat16 [25600, 1792], P('dp', 'mp')
- input_grad: bfloat16 [25600, 1792], P('dp', 'mp')
- new_master: float32 [1792, 4, 1792], P('dp', None, 'mp')
- new_moment_one: float32 [1792, 4, 1792], P('dp', None, 'mp')
- new_moment_two: float32 [1792, 4, 1792], P('dp', None, 'mp')
- new_gain: float32 [1792], replicated
- new_bias: float32 [1792], replicated
- new_norm_moment_one: float32 [2, 1792], replicated
- new_norm_moment_two: float32 [2, 1792], replicated
The draws below stay inside these ranges and needn't reach their ends.
Inputs may be any that keep to these rules, and one draw needn't show every extreme that they name: `tokens_per_image`: A square number s * s; some group has exactly 400. image_count[g] * tokens_per_image[g] is at most 400 for every group g.
All inputs are finite; a program needn't handle non-finite values.
Results may differ from the reference program's by a relative error of at most 0.0085.
Values may be sent and summed in bfloat16 or wider, within the bound.
A program may use at most 192 MiB of HBM per device.

```python
import math
import jax
import jax.numpy as jnp
from jax import lax

D = 1792
HEADS = 16
HEAD_DIM = 112
GRID = 20
TOK_DEV = 400
GROUPS = 64
TOKENS = 25600
HD = 1792
N_DP = 64
N_MP = 2


def group_plan(key):
    folded = jax.random.fold_in(key, 11)
    side_key, pick_key, count_key = jax.random.split(folded, 3)
    lowest = max(2, GRID // 5)
    side_cells = jax.random.randint(side_key, (GROUPS,), lowest, GRID + 1)
    chosen = jax.random.randint(pick_key, (), 0, GROUPS)
    coarse = (chosen + 1) % GROUPS
    places = jnp.arange(GROUPS)
    side_cells = jnp.where(places == chosen, GRID, side_cells)
    side_cells = jnp.where(places == coarse, lowest, side_cells)
    lengths = side_cells * side_cells
    most_images = GRID * GRID // lengths
    least_images = jnp.maximum(1, most_images // 2)
    counts = jax.random.randint(count_key, (GROUPS,), least_images, most_images + 1)
    counts = jnp.where(places == coarse, most_images, counts)
    return (counts.astype(jnp.int32), lengths.astype(jnp.int32))


def draw_image_count(key, part):
    return group_plan(key)[0]


def draw_tokens_per_image(key, part):
    return group_plan(key)[1]


def draw_master(key, part):
    width_all = HEADS * HEAD_DIM
    first_key = jax.random.fold_in(jax.random.fold_in(key, 23), 0)
    drawn_all = jax.random.normal(first_key, (D, 4, width_all), jnp.float32) * D ** (-0.5)
    return drawn_all


def shard_levels(key, dims, shards, low, high):
    level, own = 1.0, jax.random.fold_in(key, 6)
    for axis_at, shards_of in shards:
        heights = jnp.exp(jax.random.uniform(jax.random.fold_in(own, axis_at), (shards_of,), jnp.float32, low / len(shards), high / len(shards)))
        level = level * jnp.repeat(heights, dims[axis_at] // shards_of).reshape([-1 if axis == axis_at else 1 for axis in range(len(dims))])
    return level


def scatter_about(key, shape, scale, bound, shards=(), kind=jnp.bfloat16):
    entries = scale * jax.random.normal(key, shape, jnp.float32)
    if shards:
        entries = entries * shard_levels(key, shape, shards, -0.22, 0.18)
    return jnp.clip(entries, -bound, bound).astype(kind)


def setup_inputs(seed: int = 0) -> dict:
    splits = jax.random.split(jax.random.key(seed), 12)
    return {
        "tokens": scatter_about(splits[0], (TOKENS, D), 1.0, 6.0, ((0, 64), (1, 2))),
        "cotangent": scatter_about(splits[1], (TOKENS, D), 1.0, 6.0, ((0, 64), (1, 2))),
        "master": draw_master(jax.random.fold_in(splits[11], 71), 0),
        "moment_one": scatter_about(splits[3], (D, 4, HD), 0.5, 4.0, ((0, 64), (2, 2)), jnp.float32),
        "moment_two": jnp.clip(jnp.exp(math.log(1.0) - 4.6051702 * jax.random.uniform(splits[4], (D, 4, HD), jnp.float32) ** shard_levels(splits[4], (D, 4, HD), ((0, 64), (2, 2)), -0.2, 0.2)), 0.01, 1.0),
        "ln_gain": jnp.clip(1.0 + 0.18 * jax.random.normal(splits[5], (D,), jnp.float32), 0.1, 1.9),
        "ln_bias": scatter_about(splits[6], (D,), 0.5, 3.0, (), jnp.float32),
        "norm_moment_one": scatter_about(splits[7], (2, D), 0.5, 4.0, (), jnp.float32),
        "norm_moment_two": jnp.clip(jnp.exp(jax.random.uniform(splits[8], (2, D), jnp.float32, math.log(0.01), math.log(1.0))), 0.01, 1.0),
        "image_count": draw_image_count(jax.random.fold_in(splits[11], 71), 0),
        "tokens_per_image": draw_tokens_per_image(jax.random.fold_in(splits[11], 71), 0),
    }


eps_norm = 1e-06
beta_one = 0.9
beta_two = 0.95
learn_rate = 0.01
decay_rate = 0.1
adam_eps = 1e-08
step_count = 10.0

def layer_norm(row_block, gain, shift):
    values = row_block.astype(jnp.float32)
    center = lax.optimization_barrier(jnp.mean(values, axis=-1, keepdims=True))
    shifted = values - center
    spread = lax.optimization_barrier(jnp.mean(shifted * shifted, axis=-1, keepdims=True))
    inverse = lax.rsqrt(spread + eps_norm)
    normed = shifted * inverse
    return (normed, inverse, (normed * gain + shift).astype(jnp.bfloat16))

def same_image(image_here, length_here, total_rows):
    places = jnp.arange(total_rows, dtype=jnp.int32)
    live_rows = places < image_here * length_here
    labels = jnp.where(live_rows, places // length_here, jnp.int32(-1))
    return (live_rows, labels[:, None] == labels[None, :])

def half_block(normed_low, weights, allowed, grad_full):
    wide = jnp.float32
    row_count = normed_low.shape[0]
    heads_here = weights.shape[2] // HEAD_DIM
    score_scale = HEAD_DIM ** (-0.5)
    projected = jnp.einsum('td,dkh->kth', normed_low.astype(wide), weights[:, :3].astype(wide)).astype(jnp.bfloat16)
    query_rows = projected[0].reshape(row_count, heads_here, HEAD_DIM)
    key_rows = projected[1].reshape(row_count, heads_here, HEAD_DIM)
    value_rows = projected[2].reshape(row_count, heads_here, HEAD_DIM)
    scores = jnp.einsum('qhd,khd->hqk', query_rows.astype(wide), key_rows.astype(wide)) * score_scale
    scores = jnp.where(allowed[None], scores, -1e+30)
    row_max = lax.optimization_barrier(jnp.max(scores, axis=-1, keepdims=True))
    raised = jnp.exp(scores - row_max)
    prob_full = raised / lax.optimization_barrier(jnp.sum(raised, axis=-1, keepdims=True))
    prob_half = prob_full.astype(jnp.bfloat16)
    mixed = jnp.einsum('hqk,khd->qhd', prob_half.astype(wide), value_rows.astype(wide)).astype(jnp.bfloat16)
    mixed = mixed.reshape(row_count, heads_here * HEAD_DIM)
    out_weight = weights[:, 3]
    out_part = jnp.einsum('th,dh->td', mixed.astype(wide), out_weight.astype(wide))
    out_grad = jnp.einsum('td,th->dh', grad_full.astype(wide), mixed.astype(wide))
    mixed_grad = jnp.dot(grad_full, out_weight, preferred_element_type=jnp.float32).astype(jnp.bfloat16)
    mixed_grad = mixed_grad.reshape(row_count, heads_here, HEAD_DIM)
    prob_grad = jnp.einsum('qhd,khd->hqk', mixed_grad.astype(wide), value_rows.astype(wide))
    value_grad = jnp.einsum('hqk,qhd->khd', prob_half.astype(wide), mixed_grad.astype(wide)).astype(jnp.bfloat16)
    delta = lax.optimization_barrier(jnp.sum(prob_full * prob_grad, axis=-1, keepdims=True))
    score_grad = (prob_full * (prob_grad - delta) * score_scale).astype(jnp.bfloat16)
    query_grad = jnp.einsum('hqk,khd->qhd', score_grad.astype(wide), key_rows.astype(wide)).astype(jnp.bfloat16)
    key_grad = jnp.einsum('hqk,qhd->khd', score_grad.astype(wide), query_rows.astype(wide)).astype(jnp.bfloat16)
    proj_grad = jnp.stack([query_grad, key_grad, value_grad]).reshape(3, row_count, heads_here * HEAD_DIM)
    norm_grad = jnp.einsum('kth,dkh->td', proj_grad.astype(wide), weights[:, :3].astype(wide))
    inner_grad = jnp.einsum('td,kth->dkh', normed_low.astype(wide), proj_grad.astype(wide))
    grads = jnp.concatenate([inner_grad, out_grad[:, None]], axis=1)
    return (out_part, norm_grad, grads)

def adam_update(weight_now, moment_first, moment_second, gradient, decay):
    first_new = beta_one * moment_first + (1.0 - beta_one) * gradient
    second_new = beta_two * moment_second + (1.0 - beta_two) * gradient * gradient
    first_hat = first_new / (1.0 - beta_one ** step_count)
    second_hat = second_new / (1.0 - beta_two ** step_count)
    weight_new = weight_now - learn_rate * (first_hat / (jnp.sqrt(second_hat) + adam_eps) + decay * weight_now)
    return (weight_new, first_new, second_new)

def reference(tokens, cotangent, master, moment_one, moment_two, ln_gain, ln_bias, norm_moment_one, norm_moment_two, image_count, tokens_per_image):
    weights = master.astype(jnp.bfloat16)
    width_here = HEADS * HEAD_DIM // N_MP
    token_blocks = tokens.reshape(N_DP, TOK_DEV, D)
    cot_blocks = cotangent.reshape(N_DP, TOK_DEV, D)

    def one_group(carry, inputs):
        grad_total, gain_total, bias_total = carry
        block_rows, cot_rows, image_here, length_here = inputs
        normed, inverse, normed_low = layer_norm(block_rows, ln_gain, ln_bias)
        live_rows, allowed = same_image(image_here, length_here, TOK_DEV)
        grad_full = jnp.where(live_rows[:, None], cot_rows, jnp.zeros_like(cot_rows))
        out_sum = jnp.zeros((TOK_DEV, D), jnp.float32)
        input_sum = jnp.zeros((TOK_DEV, D), jnp.float32)
        pieces = []
        for shard_index in range(N_MP):
            part_weights = weights[:, :, shard_index * width_here:(shard_index + 1) * width_here]
            out_part, norm_grad, grads = half_block(normed_low, part_weights, allowed, grad_full)
            out_sum = out_sum + lax.optimization_barrier(out_part.astype(jnp.bfloat16)).astype(jnp.float32)
            gain_total = gain_total + lax.optimization_barrier(jnp.sum(norm_grad * normed, axis=0))
            bias_total = bias_total + lax.optimization_barrier(jnp.sum(norm_grad, axis=0))
            scaled = norm_grad * ln_gain
            input_part = inverse * (scaled - lax.optimization_barrier(jnp.mean(scaled, axis=-1, keepdims=True)) - normed * lax.optimization_barrier(jnp.mean(scaled * normed, axis=-1, keepdims=True)))
            input_sum = input_sum + lax.optimization_barrier(input_part.astype(jnp.bfloat16)).astype(jnp.float32)
            pieces.append(grads)
        grad_total = grad_total + jnp.concatenate(pieces, axis=2)
        block_out = (block_rows.astype(jnp.float32) + out_sum).astype(jnp.bfloat16)
        input_grad = (grad_full.astype(jnp.float32) + input_sum).astype(jnp.bfloat16)
        return ((grad_total, gain_total, bias_total), (block_out, input_grad))
    start_carry = (jnp.zeros((D, 4, HEADS * HEAD_DIM), jnp.float32), jnp.zeros((D,), jnp.float32), jnp.zeros((D,), jnp.float32))
    totals, outputs = lax.scan(one_group, start_carry, (token_blocks, cot_blocks, image_count, tokens_per_image))
    grad_total, gain_total, bias_total = totals
    block_out = outputs[0].reshape(N_DP * TOK_DEV, D)
    input_grad = outputs[1].reshape(N_DP * TOK_DEV, D)
    weight_grad = grad_total / N_DP
    new_master, new_moment_one, new_moment_two = adam_update(master, moment_one, moment_two, weight_grad, decay_rate)
    norm_param_grad = jnp.stack([gain_total, bias_total]) / N_DP
    stacked_params = jnp.stack([ln_gain, ln_bias])
    new_norm, new_norm_moment_one, new_norm_moment_two = adam_update(stacked_params, norm_moment_one, norm_moment_two, norm_param_grad, 0.0)
    return (block_out, input_grad, new_master, new_moment_one, new_moment_two, new_norm[0], new_norm[1], new_norm_moment_one, new_norm_moment_two)
```

```python
import functools

import jax
import jax.numpy as jnp
from jax import lax
from jax.experimental import pallas as pl
from jax.experimental.pallas import tpu as pltpu
from jax.sharding import Mesh
from jax.sharding import PartitionSpec as P

HEADS = 8
HEAD_DIM = 112
PAD = 128
ROWS = 400
DIM = 1792
COLS = 896
BLOCK = 56
SHARD = 28
GROUPS = 64
DP = ("dp_0", "dp_1", "dp_2", "dp_3")
AXES = DP + ("mp",)
MESH = pl.DeviceIdType.MESH
N_SEMS = 224

eps_norm = 1e-06
beta_one = 0.9
beta_two = 0.95
learn_rate = 0.01
decay_rate = 0.1
adam_eps = 1e-08
step_count = 10.0

bf16 = jnp.bfloat16
f32 = jnp.float32

ORDER = (0, -1, 1, 2)
LEFT = pl.ds(0, 512)
RIGHT = pl.ds(512, 384)


def nt_dot(a, b):
    return lax.dot_general(a, b, (((1,), (1,)), ((), ())), preferred_element_type=f32)


def tn_dot(a, b):
    return lax.dot_general(a, b, (((0,), (0,)), ((), ())), preferred_element_type=f32)


def mod4(v):
    return lax.rem(v + 8, 4)


def block_kernel(
    tok, cot, wl, gain, bias, count, length,
    bo, ig, gout, ngout,
    W, xf, gf, xn, tn, tg, tnr, tgr, heads, outs, D, Dr,
    part, ra, sb, rb, rf, yb, yr, fs, fr, wsib, ops, opr, ips, ipr,
    mean_s, inv_s, nsrc, nr,
    ss, rs,
):
    z, yh, x, c, m = [lax.axis_index(a) for a in AXES]
    big, small = x + c * (z - x), z + c * (x - z)
    home, away = c == yh, c != yh

    def big_dev(d):
        return (mod4(z + c * d), yh, mod4(x + (1 - c) * d), c, m)

    def small_dev(d):
        return (mod4(z + (1 - c) * d), yh, mod4(x + c * d), c, m)

    sib = (z, yh, x, 1 - c, m)
    ypart = (z, 1 - yh, x, c, m)
    mate = (z, yh, x, c, 1 - m)

    index, pending = {}, []

    def message(name, src, dst, dev):
        k = index.setdefault(name, len(index))
        assert k < N_SEMS
        return pltpu.make_async_remote_copy(
            src_ref=src, dst_ref=dst, send_sem=ss.at[k], recv_sem=rs.at[k],
            device_id=dev, device_id_type=MESH,
        )

    def send(name, src, dst, dev):
        copy = message(name, src, dst, dev)
        copy.start()
        pending.append((copy.wait_send, None))

    def send_inside(when, name, build):
        message(name, *build()).start()
        pending.append((lambda: message(name, *build()).wait_send(), when))

    def recv(name, dst):
        message(name, dst, dst, sib).wait_recv()

    barrier = pltpu.get_barrier_semaphore()
    partners = (sib, ypart, mate, big_dev(1), big_dev(-1), small_dev(1), small_dev(-1))
    for dev in partners:
        pl.semaphore_signal(barrier, inc=1, device_id=dev, device_id_type=MESH)
    pl.semaphore_wait(barrier, len(partners))

    def cols(half):
        return pl.ds(pl.multiple_of(half * COLS, 128), COLS)

    def blk(i, j, cc=c):
        return i * (1 + 7 * cc) + j * (8 - 7 * cc) + 4 * cc

    own = blk(big, small)

    def spread(p, n, b):
        send(("b+", p, n), W.at[p, b], W.at[p, b], big_dev(1))
        send(("b-", p, n), W.at[p, b], W.at[p, b], big_dev(-1))
        send(("sib", p, n), W.at[p, b], W.at[p, b], sib)

    def gather_first(p):
        @pl.when(away)
        def _():
            send_inside(away, ("w", p), lambda: (wl.at[p], wsib.at[p], sib))

    def gather_own(p):
        @pl.when(home)
        def _():
            recv(("w", p), wsib.at[p])
            mine, other = wl[p].astype(f32), wsib[p].astype(f32)
            low = jnp.where(c == 0, mine, other)
            high = jnp.where(c == 0, other, mine)
            W[p, own] = jnp.concatenate([low, high], axis=0).astype(bf16)
            send_inside(home, ("y", p), lambda: (W.at[p, own], W.at[p, own], ypart))

        @pl.when(away)
        def _():
            recv(("y", p), W.at[p, own])

        send(("s+", p), W.at[p, own], W.at[p, own], small_dev(1))
        send(("s-", p), W.at[p, own], W.at[p, own], small_dev(-1))
        spread(p, 0, own)

    def gather_small(p):
        low, high, far = [blk(big, mod4(small + d)) for d in (-1, 1, 2)]
        recv(("s+", p), W.at[p, low])
        half = W.at[p, low, :, LEFT]
        send(("sf+", p), half, half, small_dev(1))
        spread(p, 1, low)
        recv(("s-", p), W.at[p, high])
        half = W.at[p, high, :, RIGHT]
        send(("sf-", p), half, half, small_dev(-1))
        spread(p, 2, high)
        recv(("sf+", p), W.at[p, far, :, LEFT])
        recv(("sf-", p), W.at[p, far, :, RIGHT])
        spread(p, 3, far)

    def gather_big(p):
        for n, d in enumerate(ORDER):
            j = mod4(small + d)
            b = blk(mod4(big - 1), j)
            recv(("b+", p, n), W.at[p, b])
            if n < 2:
                send(("f+", p, n), W.at[p, b], W.at[p, b], big_dev(1))
            send(("sib", p, 4 + n), W.at[p, b], W.at[p, b], sib)
            b = blk(mod4(big + 1), j)
            recv(("b-", p, n), W.at[p, b])
            if n >= 2:
                send(("f-", p, n), W.at[p, b], W.at[p, b], big_dev(-1))
            send(("sib", p, 8 + n), W.at[p, b], W.at[p, b], sib)

    def gather_far(p):
        for n, d in enumerate(ORDER):
            b = blk(mod4(big + 2), mod4(small + d))
            recv(("f+" if n < 2 else "f-", p, n), W.at[p, b])
            send(("sib", p, 12 + n), W.at[p, b], W.at[p, b], sib)

    def gather_done(p):
        for k, step in enumerate((0, -1, 1, 2)):
            for n, d in enumerate(ORDER):
                b = blk(mod4(small + step), mod4(big + d), 1 - c)
                recv(("sib", p, 4 * k + n), W.at[p, b])

    def weight(p):
        return W[p].reshape(DIM, COLS)

    def flip(src, dst):
        for h in range(2):
            dst[pl.ds(16 * h, 16)] = src[:, h * COLS : (h + 1) * COLS].T.reshape(16, BLOCK, ROWS)

    def to_sibling(name, src, dst):
        for k in range(4):
            send((name, k), src.at[pl.ds(8 * k + 4 * (1 - c), 4)], dst.at[pl.ds(4 * k, 4)], sib)

    def from_sibling(name, dst):
        for k in range(4):
            recv((name, k), dst.at[pl.ds(4 * k, 4)])

    live_count = (count[0] * length[0]).astype(f32)

    def live_rows(start, size):
        at = lax.broadcasted_iota(jnp.int32, (size, 1), 0).astype(f32) + float(start)
        return at < live_count

    def norm():
        def body(n, _):
            r = pl.ds(pl.multiple_of(n * 80, 16), 80)
            values = xf[r, :].astype(f32)
            center = jnp.mean(values, axis=-1, keepdims=True)
            shifted = values - center
            spread_ = jnp.mean(shifted * shifted, axis=-1, keepdims=True)
            inverse = lax.rsqrt(spread_ + eps_norm)
            mean_s[r, :] = center
            inv_s[r, :] = inverse
            xn[r, :] = (shifted * inverse * gain[...] + bias[...]).astype(bf16)
            return 0

        lax.fori_loop(0, ROWS // 80, body, 0)

    def split_heads(value, dst):
        low = value.astype(bf16)
        for h in range(HEADS):
            dst[h, :, :HEAD_DIM] = low[:, h * HEAD_DIM : (h + 1) * HEAD_DIM]
            dst[h, :, HEAD_DIM:] = jnp.zeros((ROWS, PAD - HEAD_DIM), bf16)

    def project(p, rows):
        split_heads(jnp.dot(rows[...], weight(p), preferred_element_type=f32), heads.at[p])

    scale = HEAD_DIM**-0.5

    def label(at):
        per = length[0].astype(f32)
        return jnp.where(at < live_count, jnp.floor((at + 0.5) / per), -1.0)

    def attention():
        down = lax.broadcasted_iota(jnp.int32, (ROWS, 1), 0).astype(f32)
        along = lax.broadcasted_iota(jnp.int32, (1, ROWS), 1).astype(f32)
        down, along = label(down), label(along)

        def body(h, _):
            qh, kh, vh, gh = heads[0, h], heads[1, h], heads[2, h], heads[3, h]
            s = jnp.where(down == along, nt_dot(qh, kh) * scale, -1e30)
            e = jnp.exp(s - jnp.max(s, axis=1, keepdims=True))
            prob = e * (1.0 / jnp.sum(e, axis=1, keepdims=True))
            low = prob.astype(bf16)
            outs[3, h] = jnp.dot(low, vh, preferred_element_type=f32).astype(bf16)
            dp = nt_dot(gh, vh)
            outs[2, h] = tn_dot(low, gh).astype(bf16)
            delta = jnp.sum(prob * dp, axis=1, keepdims=True)
            ds = (prob * (dp - delta) * scale).astype(bf16)
            outs[0, h] = jnp.dot(ds, kh, preferred_element_type=f32).astype(bf16)
            outs[1, h] = tn_dot(ds, qh).astype(bf16)
            return 0

        lax.fori_loop(0, HEADS, body, 0)

    def merge(p):
        for h in range(HEADS):
            D[p, :, h * HEAD_DIM : (h + 1) * HEAD_DIM] = outs[p, h][:, :HEAD_DIM]
        send(("D", p), D.at[p], Dr.at[p], sib)

    def half_weight(p, half):
        return W[p, pl.ds(16 * half, 16)].reshape(COLS, COLS)

    def out_projection():
        mixed = D[3]
        ops[...] = nt_dot(mixed, half_weight(3, 1 - m)).astype(bf16)
        send(("op",), ops, opr, mate)
        bo[...] = nt_dot(mixed, half_weight(3, m)).astype(bf16)

    def norm_backward():
        gain_sum = jnp.zeros((1, DIM), f32)
        bias_sum = jnp.zeros((1, DIM), f32)
        for start, size in ((0, 208), (208, 192)):
            r = pl.ds(start, size)
            ng = nt_dot(D[0, r, :], weight(0)) + nt_dot(D[1, r, :], weight(1))
            ng = ng + nt_dot(D[2, r, :], weight(2))
            normed = (xf[r, :].astype(f32) - mean_s[r, :]) * inv_s[r, :]
            gain_sum = gain_sum + jnp.sum(ng * normed, axis=0, keepdims=True)
            bias_sum = bias_sum + jnp.sum(ng, axis=0, keepdims=True)
            a = ng * gain[...]
            first = jnp.mean(a, axis=-1, keepdims=True)
            second = jnp.mean(a * normed, axis=-1, keepdims=True)
            ip = (inv_s[r, :] * (a - first - normed * second)).astype(bf16)
            ips[r, :] = jnp.where(m == 0, ip[:, COLS:], ip[:, :COLS])
            ig[r, :] = jnp.where(m == 0, ip[:, :COLS], ip[:, COLS:])
        send(("ip",), ips, ipr, mate)
        nsrc[0, 0:1, :] = gain_sum
        nsrc[0, 1:2, :] = bias_sum
        send(("n", 0), nsrc.at[0], nr.at[0, 0], sib)

    def norm_ring(k, pos, dev):
        send(("n+", k), nsrc.at[k], nr.at[k, pos], dev(1))
        send(("n-", k), nsrc.at[k], nr.at[k, pos], dev(-1))
        recv(("n+", k), nr.at[k, mod4(pos - 1)])
        send(("nf", k), nr.at[k, mod4(pos - 1)], nr.at[k, mod4(pos - 1)], dev(1))
        nr[k, pos] = nsrc[k]
        recv(("n-", k), nr.at[k, mod4(pos + 1)])
        recv(("nf", k), nr.at[k, mod4(pos + 2)])
        nsrc[k + 1] = (nr[k, 0] + nr[k, 1]) + (nr[k, 2] + nr[k, 3])

    def x_dev(d):
        return (z, yh, mod4(x + d), c, m)

    def z_dev(d):
        return (mod4(z + d), yh, x, c, m)

    def norm_sum_chip():
        recv(("n", 0), nr.at[0, 0])
        nsrc[1] = nsrc[0] + nr[0, 0]

    def norm_pair(k, dev):
        send(("n", k), nsrc.at[k], nr.at[k, 0], dev)
        recv(("n", k), nr.at[k, 0])
        nsrc[k + 1] = nsrc[k] + nr[k, 0]

    def grad_chunk(p, i):
        own_rows, sib_rows = (tg, tgr) if p == 3 else (tn, tnr)
        a = jnp.concatenate([own_rows[blk(i, j)] for j in range(4)], axis=0)
        b = jnp.concatenate([sib_rows[i * (1 + 3 * c) + j * (4 - 3 * c)] for j in range(4)], axis=0)
        v = jnp.dot(a, D[p], preferred_element_type=f32)
        v = v + jnp.dot(b, Dr[p], preferred_element_type=f32)
        part[p, i] = v.astype(bf16).reshape(4, BLOCK, COLS)

    lo, hi = pl.ds(0, 2), pl.ds(2, 2)
    nxt, prv, opp = mod4(big + 1), mod4(big - 1), mod4(big + 2)

    def grads(p):
        grad_chunk(p, opp)
        send(("1a", p), part.at[p, opp, lo], ra.at[p, 0], big_dev(1))
        send(("1b", p), part.at[p, opp, hi], ra.at[p, 1], big_dev(-1))
        grad_chunk(p, nxt)
        send(("2b", p), part.at[p, nxt, hi], ra.at[p, 2], big_dev(1))
        grad_chunk(p, prv)
        send(("2a", p), part.at[p, prv, lo], ra.at[p, 3], big_dev(-1))
        grad_chunk(p, big)

    def wide_add(p):
        recv(("1a", p), ra.at[p, 0])
        part[p, nxt, lo] = (part[p, nxt, lo].astype(f32) + ra[p, 0].astype(f32)).astype(bf16)
        send(("3a", p), part.at[p, nxt, lo], ra.at[p, 4], big_dev(1))
        recv(("1b", p), ra.at[p, 1])
        part[p, prv, hi] = (part[p, prv, hi].astype(f32) + ra[p, 1].astype(f32)).astype(bf16)
        send(("3b", p), part.at[p, prv, hi], ra.at[p, 5], big_dev(-1))

    def wide_sum(p):
        recv(("2b", p), ra.at[p, 2])
        recv(("2a", p), ra.at[p, 3])
        recv(("3a", p), ra.at[p, 4])
        recv(("3b", p), ra.at[p, 5])
        v = part[p, big, lo].astype(f32) + ra[p, 3].astype(f32) + ra[p, 4].astype(f32)
        sb[p, lo] = v.astype(bf16)
        v = part[p, big, hi].astype(f32) + ra[p, 2].astype(f32) + ra[p, 5].astype(f32)
        sb[p, hi] = v.astype(bf16)

    snx, spv, sop = mod4(small + 1), mod4(small - 1), mod4(small + 2)

    def narrow_send(q, p0, p1):
        send(("4a", q), sb.at[p0, sop], rb.at[q, 0], small_dev(1))
        send(("4b", q), sb.at[p1, sop], rb.at[q, 1], small_dev(-1))
        send(("5b", q), sb.at[p1, snx], rb.at[q, 2], small_dev(1))
        send(("5a", q), sb.at[p0, spv], rb.at[q, 3], small_dev(-1))

    def narrow_add(q, p0, p1):
        recv(("4a", q), rb.at[q, 0])
        sb[p0, snx] = (sb[p0, snx].astype(f32) + rb[q, 0].astype(f32)).astype(bf16)
        send(("6a", q), sb.at[p0, snx], rb.at[q, 4], small_dev(1))
        recv(("4b", q), rb.at[q, 1])
        sb[p1, spv] = (sb[p1, spv].astype(f32) + rb[q, 1].astype(f32)).astype(bf16)
        send(("6b", q), sb.at[p1, spv], rb.at[q, 5], small_dev(-1))

    def narrow_sum(q, p0, p1):
        recv(("5b", q), rb.at[q, 2])
        recv(("5a", q), rb.at[q, 3])
        recv(("6a", q), rb.at[q, 4])
        recv(("6b", q), rb.at[q, 5])
        rf[p0] = sb[p0, small].astype(f32) + rb[q, 3].astype(f32) + rb[q, 4].astype(f32)
        rf[p1] = sb[p1, small].astype(f32) + rb[q, 2].astype(f32) + rb[q, 5].astype(f32)
        for p in (p0, p1):
            over_y(p)

    def over_y(p):
        @pl.when(away)
        def _():
            yb[p] = rf[p].astype(bf16)
            send_inside(away, ("Y", p), lambda: (yb.at[p], yr.at[p], ypart))

    def finish(p):
        @pl.when(home)
        def _():
            recv(("Y", p), yr.at[p])
            v = rf[p] + yr[p].astype(f32)
            low, high = v[:SHARD], v[SHARD:]
            gout[p] = jnp.where(c == 0, low, high)
            fs[p] = jnp.where(c == 0, high, low)
            send_inside(home, ("F", p), lambda: (fs.at[p], fr.at[p], sib))

    def finish_other(p):
        @pl.when(away)
        def _():
            recv(("F", p), fr.at[p])
            gout[p] = fr[p]

    send(("tok",), tok, xf.at[:, cols(m)], mate)
    for p in range(4):
        gather_first(p)
    xf[:, cols(m)] = tok[...]
    gf[:, cols(m)] = cot[...]
    gather_own(0)
    gather_small(0)
    gather_own(1)
    gather_small(1)
    gather_big(0)
    gather_own(2)
    gather_far(0)
    recv(("tok",), xf.at[:, cols(1 - m)])
    send(("cot",), cot, gf.at[:, cols(m)], mate)
    gather_small(2)
    norm()
    gather_big(1)
    gather_own(3)
    flip(xn, tn)
    to_sibling("tn", tn, tnr)
    gather_far(1)
    gather_small(3)
    gather_done(0)
    project(0, xn)
    gather_big(2)
    gather_done(1)
    gather_far(2)
    project(1, xn)
    gather_big(3)
    gather_done(2)
    gather_far(3)
    project(2, xn)
    recv(("cot",), gf.at[:, cols(1 - m)])
    gf[...] = jnp.where(live_rows(0, ROWS), gf[...].astype(f32), 0.0).astype(bf16)
    flip(gf, tg)
    to_sibling("tg", tg, tgr)
    gather_done(3)
    project(3, gf)
    attention()
    for p in (3, 2, 0, 1):
        merge(p)
    from_sibling("tn", tnr)
    from_sibling("tg", tgr)
    recv(("D", 3), Dr.at[3])
    grads(3)
    out_projection()
    recv(("D", 2), Dr.at[2])
    grads(2)
    wide_add(3)
    recv(("D", 0), Dr.at[0])
    recv(("D", 1), Dr.at[1])
    norm_backward()
    wide_add(2)
    grads(0)
    wide_sum(3)
    wide_sum(2)
    narrow_send(0, 3, 2)
    grads(1)
    norm_sum_chip()
    wide_add(0)
    narrow_add(0, 3, 2)
    norm_ring(1, x, x_dev)
    wide_add(1)
    narrow_sum(0, 3, 2)
    norm_ring(2, z, z_dev)
    recv(("op",), opr)
    bo[...] = (tok[...].astype(f32) + (bo[...].astype(f32) + opr[...].astype(f32))).astype(bf16)
    norm_pair(3, mate)
    wide_sum(0)
    norm_pair(4, ypart)
    ngout[...] = nsrc[5]
    finish(3)
    finish(2)
    wide_sum(1)
    narrow_send(1, 0, 1)
    recv(("ip",), ipr)
    kept = jnp.where(live_rows(0, ROWS), cot[...].astype(f32), 0.0)
    ig[...] = (kept + (ig[...].astype(f32) + ipr[...].astype(f32))).astype(bf16)
    narrow_add(1, 0, 1)
    narrow_sum(1, 0, 1)
    finish(0)
    finish(1)
    for p in range(4):
        finish_other(p)

    for wait, when in pending:
        if when is None:
            wait()
        else:
            pl.when(when)(wait)


def run_block(tokens, cotangent, wl, gain, bias, image_count, tokens_per_image):
    vmem = pl.BlockSpec(memory_space=pltpu.VMEM)
    smem = pl.BlockSpec(memory_space=pltpu.SMEM)
    V = pltpu.VMEM
    return pl.pallas_call(
        block_kernel,
        out_shape=(
            jax.ShapeDtypeStruct((ROWS, COLS), bf16),
            jax.ShapeDtypeStruct((ROWS, COLS), bf16),
            jax.ShapeDtypeStruct((4, SHARD, COLS), f32),
            jax.ShapeDtypeStruct((2, DIM), f32),
        ),
        in_specs=[vmem] * 5 + [smem] * 2,
        out_specs=(vmem,) * 4,
        scratch_shapes=[
            V((4, 32, BLOCK, COLS), bf16),
            V((ROWS, DIM), bf16),
            V((ROWS, DIM), bf16),
            V((ROWS, DIM), bf16),
            V((32, BLOCK, ROWS), bf16),
            V((32, BLOCK, ROWS), bf16),
            V((16, BLOCK, ROWS), bf16),
            V((16, BLOCK, ROWS), bf16),
            V((4, HEADS, ROWS, PAD), bf16),
            V((4, HEADS, ROWS, PAD), bf16),
            V((4, ROWS, COLS), bf16),
            V((4, ROWS, COLS), bf16),
            V((4, 4, 4, BLOCK, COLS), bf16),
            V((4, 6, 2, BLOCK, COLS), bf16),
            V((4, 4, BLOCK, COLS), bf16),
            V((2, 6, BLOCK, COLS), bf16),
            V((4, BLOCK, COLS), f32),
            V((4, BLOCK, COLS), bf16),
            V((4, BLOCK, COLS), bf16),
            V((4, SHARD, COLS), f32),
            V((4, SHARD, COLS), f32),
            V((4, SHARD, COLS), bf16),
            V((ROWS, COLS), bf16),
            V((ROWS, COLS), bf16),
            V((ROWS, COLS), bf16),
            V((ROWS, COLS), bf16),
            V((ROWS, 1), f32),
            V((ROWS, 1), f32),
            V((6, 2, DIM), f32),
            V((5, 4, 2, DIM), f32),
            pltpu.SemaphoreType.DMA((N_SEMS,)),
            pltpu.SemaphoreType.DMA((N_SEMS,)),
        ],
        compiler_params=pltpu.CompilerParams(
            collective_id=0, has_side_effects=True, vmem_limit_bytes=67043328
        ),
        name="block",
    )(tokens, cotangent, wl, gain, bias, image_count, tokens_per_image)


def adam_update(weight_now, moment_first, moment_second, gradient, decay):
    first_new = beta_one * moment_first + (1.0 - beta_one) * gradient
    second_new = beta_two * moment_second + (1.0 - beta_two) * gradient * gradient
    first_hat = first_new / (1.0 - beta_one**step_count)
    second_hat = second_new / (1.0 - beta_two**step_count)
    weight_new = weight_now - learn_rate * (
        first_hat / (jnp.sqrt(second_hat) + adam_eps) + decay * weight_now
    )
    return (weight_new, first_new, second_new)


def shards(
    tokens,
    cotangent,
    master,
    moment_one,
    moment_two,
    ln_gain,
    ln_bias,
    norm_moment_one,
    norm_moment_two,
    image_count,
    tokens_per_image,
):
    wl = jnp.transpose(master.astype(bf16), (1, 0, 2))
    block_out, input_grad, grad, norm_sums = run_block(
        tokens, cotangent, wl, ln_gain[None], ln_bias[None], image_count, tokens_per_image
    )
    weight_grad = jnp.transpose(grad, (1, 0, 2)) / GROUPS
    new_master, new_moment_one, new_moment_two = adam_update(
        master, moment_one, moment_two, weight_grad, decay_rate
    )
    stacked_params = jnp.stack([ln_gain, ln_bias])
    new_norm, new_norm_moment_one, new_norm_moment_two = adam_update(
        stacked_params, norm_moment_one, norm_moment_two, norm_sums / GROUPS, 0.0
    )
    return (
        block_out,
        input_grad,
        new_master,
        new_moment_one,
        new_moment_two,
        new_norm[0],
        new_norm[1],
        new_norm_moment_one,
        new_norm_moment_two,
    )


def solution(mesh):
    finer = Mesh(mesh.devices.reshape(4, 2, 4, 2, mesh.shape["mp"]), AXES)
    return jax.shard_map(
        shards,
        mesh=finer,
        in_specs=(
            P(DP, "mp"),
            P(DP, "mp"),
            P(DP, None, "mp"),
            P(DP, None, "mp"),
            P(DP, None, "mp"),
            P(),
            P(),
            P(),
            P(),
            P(DP),
            P(DP),
        ),
        out_specs=(
            P(DP, "mp"),
            P(DP, "mp"),
            P(DP, None, "mp"),
            P(DP, None, "mp"),
            P(DP, None, "mp"),
            P(),
            P(),
            P(),
            P(),
        ),
        check_vma=False,
    )
```
